256 devices in a mesh: orient: 16 (over x, y_hi, core), pix: 16 (over y_lo, z).
Axes of the slice: x: 4, y: 4 (y_hi: 2, y_lo: 2; y = y_hi * 2 + y_lo), z: 8, core: 2. Of those that a mesh axis runs over, the one named last changes fastest.
Arguments:
- model: bfloat16 [12288, 65536], P('orient', 'pix'), may hold values from 0.012 to 3.32
- patterns: int32 [384, 65536], P(None, 'pix'), may hold values from 0 to 10, as said below
Outputs:
- updated: bfloat16 [12288, 65536], P('orient', 'pix')
The draws below stay inside these ranges and needn't reach their ends.
Inputs may be any that keep to these rules, and one draw needn't show every extreme that they name: `patterns`: each pattern has a brightness level of its own; its counts are whole numbers from 0 to one less than that level.
All inputs are finite; a program needn't handle non-finite values.
Results may differ from the reference program's by a relative error of at most 0.0022.
Values may be sent and summed in bfloat16 or wider, within the bound.
A program may use at most 64 MiB of HBM per device.

```python
import math
import jax
import jax.numpy as jnp
from jax import lax

ORIENT_DEV = 768
PIX = 65536
FRAMES = 384
ITERS = 1
ORIENT = 12288
N_ORIENT = 16


def draw_model(key, part):
    base_key = jax.random.fold_in(key, 31)
    jitter_key = jax.random.fold_in(key, 47)
    base = jnp.exp(jax.random.uniform(base_key, (1, PIX), jnp.float32, math.log(0.02), math.log(2.0)))
    jitter = jax.random.uniform(jitter_key, (ORIENT, PIX), jnp.float32, -1.0, 1.0)
    return (base * jnp.exp(0.5 * jitter)).astype(jnp.bfloat16)


def draw_patterns(key, part):
    level_key = jax.random.fold_in(key, 11)
    count_key = jax.random.fold_in(key, 23)
    order = jax.random.permutation(level_key, FRAMES).astype(jnp.int32)
    levels = 2 + order * 10 // FRAMES
    return jax.random.randint(count_key, (FRAMES, PIX), 0, levels[:, None]).astype(jnp.int32)


def setup_inputs(seed: int = 0) -> dict:
    streams_of = jax.random.split(jax.random.key(seed), 3)
    model = draw_model(jax.random.fold_in(streams_of[2], 71), 0)
    patterns = draw_patterns(jax.random.fold_in(streams_of[2], 71), 0)
    return dict(model=model, patterns=patterns)


prior_weight = 1.0

def reference(model, patterns):
    anneal_beta = 2.0 / math.sqrt(PIX)
    counts = patterns.astype(jnp.float32)
    stacked = model.reshape(N_ORIENT, ORIENT_DEV, PIX)

    def score_block(block):
        intensity = block.astype(jnp.float32)
        log_slices = jnp.log(intensity)
        products = lax.dot_general(log_slices, counts, (((1,), (1,)), ((), ())), precision=lax.Precision.HIGHEST, preferred_element_type=jnp.float32)
        totals = lax.optimization_barrier(jnp.sum(intensity, axis=1))
        return anneal_beta * (products - totals[:, None])
    for iteration in range(ITERS):
        scores = lax.map(score_block, stacked).reshape(ORIENT, FRAMES)
        highest = lax.optimization_barrier(jnp.max(scores, axis=0))
        weights = jnp.exp(scores - highest[None, :])
        probs = (weights / lax.optimization_barrier(jnp.sum(weights, axis=0))[None, :]).astype(jnp.bfloat16)
        probs = probs.reshape(N_ORIENT, ORIENT_DEV, FRAMES)

        def update_block(pair):
            block, block_probs = pair
            wide_probs = block_probs.astype(jnp.float32)
            numerator = jnp.dot(wide_probs, counts, precision=lax.Precision.HIGHEST, preferred_element_type=jnp.float32)
            normalizer = lax.optimization_barrier(jnp.sum(wide_probs, axis=1))
            result = (numerator + prior_weight * block.astype(jnp.float32)) / (normalizer[:, None] + prior_weight)
            return result.astype(jnp.bfloat16)
        stacked = lax.map(update_block, (stacked, probs))
    return stacked.reshape(ORIENT, PIX)
```

```python
import functools
import math

import jax
import jax.numpy as jnp
from jax import lax
from jax.experimental import pallas as pl
from jax.experimental.pallas import tpu as pltpu
from jax.sharding import PartitionSpec as P

PIX = 65536
BETA = 2.0 / math.sqrt(PIX)
MESH = pl.DeviceIdType.MESH

ROWS = 768
COLS = 4096
FRAMES = 384
KC = 512
NK = COLS // KC
NB = 3
BS = ROWS // NB
HALF = BS // 2
NZ = 8
OWN = FRAMES // NZ
NORIENT = 16


def exchange_kernel(
    model_ref,
    pat_ref,
    probs_ref,
    counts_out,
    mv,
    pv,
    cb,
    part,
    tot,
    recv,
    score,
    own_e,
    all_e,
    stat_own,
    stat_all,
    fac_own,
    fac_all,
    pat_sem,
    mod_sem,
    cnt_sem,
    rs_send,
    rs_recv,
    ag_send,
    ag_recv,
    st_send,
    st_recv,
    fc_send,
    fc_recv,
):
    o = lax.axis_index("orient")
    p = lax.axis_index("pix")
    y = p // NZ
    z = lax.rem(p, NZ)

    def pix_peer(dy, dz):
        py = lax.rem(y + dy, 2)
        pz = lax.rem(z + dz, NZ)
        return py, pz

    pix_offsets = [(dy, dz) for dz in (4, 3, 5, 2, 6, 1, 7, 0) for dy in (1, 0) if (dy, dz) != (0, 0)]
    plane_offsets = [(dy, do) for do in range(NORIENT) for dy in (1, 0) if (dy, do) != (0, 0)]

    def pat_copy(k):
        return pltpu.make_async_copy(
            pat_ref.at[:, pl.ds(k * KC, KC)], pv.at[k], pat_sem.at[k]
        )

    def mod_copy(b, k):
        return pltpu.make_async_copy(
            model_ref.at[pl.ds(b * BS, BS), pl.ds(k * KC, KC)],
            mv.at[b, k],
            mod_sem.at[b, k],
        )

    for k in range(NK):
        pat_copy(k).start()
        mod_copy(0, k).start()
    for b in range(1, NB):
        for k in range(NK):
            mod_copy(b, k).start()

    barrier = pltpu.get_barrier_semaphore()
    for dy, dz in pix_offsets:
        py, pz = pix_peer(dy, dz)
        pl.semaphore_signal(barrier, inc=1, device_id=(o, py * NZ + pz), device_id_type=MESH)
    for dy, do in plane_offsets:
        if do == 0:
            continue
        py, _ = pix_peer(dy, 0)
        pl.semaphore_signal(
            barrier, inc=1, device_id=(lax.rem(o + do, NORIENT), py * NZ + z), device_id_type=MESH
        )

    def rs_copy(b, dy, dz):
        py, pz = pix_peer(dy, dz)
        slot = dy * NZ + (NZ - dz) % NZ - 1
        return pltpu.make_async_remote_copy(
            src_ref=part.at[2 * b + py, pl.ds(pl.multiple_of(pz * OWN, 8), OWN), :],
            dst_ref=recv.at[b, slot],
            send_sem=rs_send,
            recv_sem=rs_recv.at[b],
            device_id=(o, py * NZ + pz),
            device_id_type=MESH,
        )

    ones = jnp.ones((8, 128), jnp.float32)

    for b in range(NB):
        part[2 * b] = jnp.zeros((FRAMES, HALF), jnp.float32)
        part[2 * b + 1] = jnp.zeros((FRAMES, HALF), jnp.float32)
        tot[...] = jnp.zeros_like(tot)

        def chunk(k, carry, b=b):
            mod_copy(b, k).wait()
            if b == 0:
                pat_copy(k).wait()
                cb[k] = pv[k].astype(jnp.float32).astype(jnp.bfloat16)
            x = mv[b, k].astype(jnp.float32)
            t = tot[...]
            for j in range(KC // 128):
                t = t + x[:, j * 128 : (j + 1) * 128]
            tot[...] = t
            logs = jnp.log(x)
            hi = logs.astype(jnp.bfloat16)
            lo = (logs - hi.astype(jnp.float32)).astype(jnp.bfloat16)
            c = cb[k]
            d = lax.dot_general(
                jnp.concatenate([c, c], axis=1),
                jnp.concatenate([hi, lo], axis=1),
                (((1,), (1,)), ((), ())),
                preferred_element_type=jnp.float32,
            )
            part[2 * b] += d[:, :HALF]
            part[2 * b + 1] += d[:, HALF:]
            return carry

        lax.fori_loop(0, NK, chunk, 0)
        row = lax.dot_general(
            ones,
            tot[...],
            (((1,), (1,)), ((), ())),
            precision=lax.Precision.HIGHEST,
            preferred_element_type=jnp.float32,
        )
        part[2 * b] -= row[0:1, :HALF]
        part[2 * b + 1] -= row[0:1, HALF:]
        if b == 0:
            pltpu.make_async_copy(cb, counts_out, cnt_sem).start()
            pl.semaphore_wait(barrier, len(pix_offsets) + len(plane_offsets) - 1)
        for dy, dz in pix_offsets:
            rs_copy(b, dy, dz).start()

    npix = len(pix_offsets)
    for b in range(NB):
        pltpu.make_async_copy(recv.at[b], recv.at[b], rs_recv.at[b]).wait()
        total = part[2 * b + y, pl.ds(pl.multiple_of(z * OWN, 8), OWN), :]
        for j in range(npix):
            total = total + recv[b, j]
        score[b] = BETA * total

    s = [score[b] for b in range(NB)]
    top = jnp.maximum(jnp.maximum(s[0], s[1]), s[2])
    m = jnp.max(top, axis=1, keepdims=True)
    acc = jnp.zeros((OWN, HALF), jnp.float32)
    for b in range(NB):
        e = jnp.exp(s[b] - m)
        acc = acc + e
        own_e[b] = e.astype(jnp.bfloat16)
    esum = jnp.sum(acc, axis=1, keepdims=True)
    eye = lax.broadcasted_iota(jnp.int32, (OWN, 128), 0) == lax.broadcasted_iota(
        jnp.int32, (OWN, 128), 1
    )
    m_row = jnp.sum(jnp.where(eye, m, 0.0), axis=0, keepdims=True)
    s_row = jnp.sum(jnp.where(eye, esum, 0.0), axis=0, keepdims=True)
    upper = lax.broadcasted_iota(jnp.int32, (8, 128), 0) < 4
    stat_own[...] = jnp.where(upper, m_row, s_row)

    def stat_copy(j, dy, do):
        py, _ = pix_peer(dy, 0)
        slot = dy * NORIENT + (NORIENT - do) % NORIENT - 1
        return pltpu.make_async_remote_copy(
            src_ref=stat_own,
            dst_ref=stat_all.at[slot],
            send_sem=st_send,
            recv_sem=st_recv,
            device_id=(lax.rem(o + do, NORIENT), py * NZ + z),
            device_id_type=MESH,
        )

    for j, (dy, do) in enumerate(plane_offsets):
        stat_copy(j, dy, do).start()

    def ag_copy(dy, dz):
        py, pz = pix_peer(dy, dz)
        return pltpu.make_async_remote_copy(
            src_ref=own_e,
            dst_ref=all_e.at[y * NZ + z],
            send_sem=ag_send,
            recv_sem=ag_recv,
            device_id=(o, py * NZ + pz),
            device_id_type=MESH,
        )

    for dy, dz in pix_offsets:
        ag_copy(dy, dz).start()

    nplane = len(plane_offsets)
    pltpu.make_async_copy(stat_all, stat_all, st_recv).wait()
    big = m_row
    for j in range(nplane):
        big = jnp.maximum(big, stat_all[j, 0:1, :])
    whole = s_row * jnp.exp(m_row - big)
    for j in range(nplane):
        whole = whole + stat_all[j, 4:5, :] * jnp.exp(stat_all[j, 0:1, :] - big)
    lane = lax.broadcasted_iota(jnp.int32, (1, 128), 1)
    whole = jnp.where(lane < OWN, whole, 1.0)
    factor = jnp.exp(m_row - big) / whole
    fac_own[...] = jnp.broadcast_to(factor, (8, 128))

    def fac_copy(dy, dz):
        py, pz = pix_peer(dy, dz)
        return pltpu.make_async_remote_copy(
            src_ref=fac_own,
            dst_ref=fac_all.at[y * NZ + z],
            send_sem=fc_send,
            recv_sem=fc_recv,
            device_id=(o, py * NZ + pz),
            device_id_type=MESH,
        )

    for dy, dz in pix_offsets:
        fac_copy(dy, dz).start()
    fac_all[y * NZ + z] = fac_own[...]
    all_e[y * NZ + z] = own_e[...]

    fac_sent = fac_all.at[pl.ds(0, npix)]
    e_sent = all_e.at[pl.ds(0, npix)]
    pltpu.make_async_copy(fac_sent, fac_sent, fc_recv).wait()
    pltpu.make_async_copy(e_sent, e_sent, ag_recv).wait()

    for yy in range(2):
        cols = []
        for zz in range(NZ):
            f = jnp.sum(jnp.where(eye, fac_all[yy * NZ + zz, 0:1, :], 0.0), axis=1, keepdims=True)
            cols.append(f)
        for b in range(NB):
            block = jnp.concatenate(
                [all_e[yy * NZ + zz, b].astype(jnp.float32) * cols[zz] for zz in range(NZ)], axis=0
            )
            r = (2 * b + yy) * HALF
            probs_ref[r : r + HALF, :] = block.T.astype(jnp.bfloat16)

    pltpu.make_async_copy(cb, counts_out, cnt_sem).wait()
    pltpu.make_async_copy(recv, recv, rs_send).wait()
    pltpu.make_async_copy(e_sent, e_sent, ag_send).wait()
    pltpu.make_async_copy(stat_all, stat_all, st_send).wait()
    pltpu.make_async_copy(fac_sent, fac_sent, fc_send).wait()


def update_kernel(probs_ref, counts_ref, model_ref, out_ref, inv):
    @pl.when(pl.program_id(0) == 0)
    def _():
        norm = jnp.sum(probs_ref[...].astype(jnp.float32), axis=1, keepdims=True)
        inv[...] = jnp.broadcast_to(1.0 / (norm + 1.0), inv.shape)

    num = jnp.dot(probs_ref[...], counts_ref[0], preferred_element_type=jnp.float32)
    x = model_ref[...].astype(jnp.float32)
    scale = jnp.concatenate([inv[...]] * (KC // 128), axis=1)
    out_ref[...] = ((num + x) * scale).astype(jnp.bfloat16)


def on_device(model, patterns):
    f32, bf16 = jnp.float32, jnp.bfloat16
    dma = pltpu.SemaphoreType.DMA
    probs, counts = pl.pallas_call(
        exchange_kernel,
        name="exchange",
        out_shape=(
            jax.ShapeDtypeStruct((ROWS, FRAMES), bf16),
            jax.ShapeDtypeStruct((NK, FRAMES, KC), bf16),
        ),
        in_specs=[pl.BlockSpec(memory_space=pl.ANY)] * 2,
        out_specs=(
            pl.BlockSpec(memory_space=pltpu.VMEM),
            pl.BlockSpec(memory_space=pl.ANY),
        ),
        scratch_shapes=[
            pltpu.VMEM((NB, NK, BS, KC), bf16),
            pltpu.VMEM((NK, FRAMES, KC), jnp.int32),
            pltpu.VMEM((NK, FRAMES, KC), bf16),
            pltpu.VMEM((2 * NB, FRAMES, HALF), f32),
            pltpu.VMEM((BS, 128), f32),
            pltpu.VMEM((NB, 15, OWN, HALF), f32),
            pltpu.VMEM((NB, OWN, HALF), f32),
            pltpu.VMEM((NB, OWN, HALF), bf16),
            pltpu.VMEM((2 * NZ, NB, OWN, HALF), bf16),
            pltpu.VMEM((8, 128), f32),
            pltpu.VMEM((31, 8, 128), f32),
            pltpu.VMEM((8, 128), f32),
            pltpu.VMEM((2 * NZ, 8, 128), f32),
            dma((NK,)),
            dma((NB, NK)),
            dma,
            dma,
            dma((NB,)),
            dma,
            dma,
            dma,
            dma,
            dma,
            dma,
        ],
        compiler_params=pltpu.CompilerParams(
            collective_id=0, has_side_effects=True, vmem_limit_bytes=40 * 1024 * 1024
        ),
    )(model, patterns)
    return pl.pallas_call(
        update_kernel,
        name="update",
        grid=(NK,),
        out_shape=jax.ShapeDtypeStruct((ROWS, COLS), bf16),
        in_specs=[
            pl.BlockSpec((ROWS, FRAMES), lambda i: (0, 0)),
            pl.BlockSpec((1, FRAMES, KC), lambda i: (i, 0, 0)),
            pl.BlockSpec((ROWS, KC), lambda i: (0, i)),
        ],
        out_specs=pl.BlockSpec((ROWS, KC), lambda i: (0, i)),
        scratch_shapes=[pltpu.VMEM((ROWS, 128), f32)],
        compiler_params=pltpu.CompilerParams(vmem_limit_bytes=20 * 1024 * 1024),
    )(probs, counts, model)


def solution(mesh):
    placed = (P("orient", "pix"), P(None, "pix"))
    return jax.shard_map(
        on_device, mesh=mesh, in_specs=placed, out_specs=P("orient", "pix"), check_vma=False
    )
```

```python
import math

import jax
import jax.numpy as jnp
from jax import lax
from jax.experimental import pallas as pl
from jax.experimental.pallas import tpu as pltpu
from jax.sharding import PartitionSpec as P

PIX = 65536
BETA = 2.0 / math.sqrt(PIX)
MESH = pl.DeviceIdType.MESH

ROWS = 768
COLS = 4096
FRAMES = 384
KC = 512
NK = COLS // KC
NB = 3
BS = ROWS // NB
NZ = 8
OWN = FRAMES // NZ
NORIENT = 16
UNROLL = 4

RS_HOPS = ((4, 3), (3, 4), (4, 3))
AG_HOPS = ((4, 3), (3, 4), (4, 3))


def exchange_kernel(
    model_ref,
    pat_ref,
    probs_ref,
    cb,
    mv,
    pv,
    part,
    tot,
    recv,
    y_out,
    y_in,
    all_e,
    stat_own,
    stat_all,
    fac_own,
    fac_all,
    pat_sem,
    mod_sem,
    rs_send,
    rs_recv,
    y_send,
    y_recv,
    ag_send,
    ag_recv,
    st_send,
    st_recv,
    fc_send,
    fc_recv,
):
    o = lax.axis_index("orient")
    p = lax.axis_index("pix")
    y = p // NZ
    z = lax.rem(p, NZ)

    def at_z(dz):
        return (o, y * NZ + lax.rem(z + dz + NZ, NZ))

    y_peer = (o, (1 - y) * NZ + z)
    orient_peers = [(do, (lax.rem(o + do, NORIENT), p)) for do in range(1, NORIENT)]

    def pat_copy(k):
        return pltpu.make_async_copy(
            pat_ref.at[:, pl.ds(k * KC, KC)], pv.at[k], pat_sem.at[k]
        )

    def mod_copy(b, k):
        return pltpu.make_async_copy(
            model_ref.at[pl.ds(b * BS, BS), pl.ds(k * KC, KC)],
            mv.at[b, k],
            mod_sem.at[b, k],
        )

    for k in range(NK):
        pat_copy(k).start()
        mod_copy(0, k).start()
    for b in range(1, NB):
        for k in range(NK):
            mod_copy(b, k).start()

    barrier = pltpu.get_barrier_semaphore()
    for dz in range(1, NZ):
        pl.semaphore_signal(barrier, inc=1, device_id=at_z(dz), device_id_type=MESH)
    pl.semaphore_signal(barrier, inc=1, device_id=y_peer, device_id_type=MESH)
    for _, peer in orient_peers:
        pl.semaphore_signal(barrier, inc=1, device_id=peer, device_id_type=MESH)

    def own_part(b, c):
        row = pl.multiple_of(lax.rem(c + NZ, NZ) * OWN, 8)
        return part.at[b, pl.ds(row, OWN), :]

    def rs_slot(b, way, step):
        return sum(sum(h) for h in RS_HOPS[:b]) + (RS_HOPS[b][0] if way else 0) + step - 1

    def rs_copy(b, way, step):
        hops = RS_HOPS[b][way]
        sign = 1 if way else -1
        slot = rs_slot(b, way, step)
        left = hops - step + 1
        src = own_part(b, z + sign * left) if step == 1 else recv.at[slot - 1]
        return pltpu.make_async_remote_copy(
            src_ref=src,
            dst_ref=recv.at[slot],
            send_sem=rs_send,
            recv_sem=rs_recv.at[slot],
            device_id=at_z(sign),
            device_id_type=MESH,
        )

    def rs_start(b):
        for way in range(2):
            rs_copy(b, way, 1).start()

    def rs_step(b, step):
        for way in range(2):
            hops = RS_HOPS[b][way]
            if step > hops:
                continue
            rs_copy(b, way, step).wait_recv()
            if step < hops:
                sign = 1 if way else -1
                slot = rs_slot(b, way, step)
                recv[slot] += own_part(b, z + sign * (hops - step))[...]
                rs_copy(b, way, step + 1).start()

    def y_copy(b):
        return pltpu.make_async_remote_copy(
            src_ref=y_out.at[b],
            dst_ref=y_in.at[b],
            send_sem=y_send,
            recv_sem=y_recv.at[b],
            device_id=y_peer,
            device_id_type=MESH,
        )

    def rs_end(b):
        low = recv[rs_slot(b, 0, RS_HOPS[b][0])]
        high = recv[rs_slot(b, 1, RS_HOPS[b][1])]
        y_out[b] = own_part(b, z)[...] + (low + high)
        y_copy(b).start()

    ones = jnp.ones((8, 128), jnp.float32)

    def chunk(b, k):
        if b == 0:
            mod_copy(b, k).wait()
            pat_copy(k).wait()
            cb[k] = pv[k].astype(jnp.float32).astype(jnp.bfloat16)
        x = mv[b, k].astype(jnp.float32)
        t = tot[b]
        for j in range(KC // 128):
            t = t + x[:, j * 128 : (j + 1) * 128]
        tot[b] = t
        logs = jnp.log(x)
        hi = logs.astype(jnp.bfloat16)
        lo = (logs - hi.astype(jnp.float32)).astype(jnp.bfloat16)
        c = cb[k]
        part[b] += lax.dot_general(
            jnp.concatenate([c, c], axis=1),
            jnp.concatenate([hi, lo], axis=1),
            (((1,), (1,)), ((), ())),
            preferred_element_type=jnp.float32,
        )

    def finish(b):
        row = lax.dot_general(
            ones,
            tot[b],
            (((1,), (1,)), ((), ())),
            precision=lax.Precision.HIGHEST,
            preferred_element_type=jnp.float32,
        )
        part[b] -= row[0:1, :]

    hooks = {(1, 4): [("step", 0, 1)], (2, 4): [("step", 0, 2), ("step", 1, 1)]}
    tail = [
        ("step", 2, 1),
        ("step", 1, 2),
        ("step", 0, 3),
        ("step", 2, 2),
        ("step", 1, 3),
        ("step", 0, 4),
        ("end", 0),
        ("step", 2, 3),
        ("step", 1, 4),
        ("end", 1),
        ("step", 2, 4),
        ("end", 2),
    ]

    def act(hook):
        kind, b = hook[0], hook[1]
        if kind == "start":
            if b == 0:
                pl.semaphore_wait(barrier, NZ + len(orient_peers))
            rs_start(b)
        elif kind == "step":
            rs_step(b, hook[2])
        else:
            rs_end(b)

    tot[...] = jnp.zeros_like(tot)
    for b in range(NB):
        part[b] = jnp.zeros((FRAMES, BS), jnp.float32)
        if b == 0:
            lax.fori_loop(0, NK, lambda k, carry: (chunk(0, k), carry)[1], 0)
        else:
            for k in range(NK):
                mod_copy(b, k).wait()
            for first in range(0, NK, UNROLL):
                for k in range(first, first + UNROLL):
                    chunk(b, k)
                for hook in hooks.get((b, first), ()):
                    act(hook)
        finish(b)
        act(("start", b))
    for hook in tail:
        act(hook)

    scores = []
    for b in range(NB):
        y_copy(b).wait_recv()
        scores.append(BETA * (y_out[b] + y_in[b]))

    m = jnp.max(jnp.maximum(jnp.maximum(scores[0], scores[1]), scores[2]), axis=1, keepdims=True)
    acc = jnp.zeros((OWN, BS), jnp.float32)
    for b in range(NB):
        e = jnp.exp(scores[b] - m)
        acc = acc + e
        all_e[z, b] = e.astype(jnp.bfloat16)
    esum = jnp.sum(acc, axis=1, keepdims=True)
    eye = lax.broadcasted_iota(jnp.int32, (OWN, 128), 0) == lax.broadcasted_iota(
        jnp.int32, (OWN, 128), 1
    )
    m_row = jnp.sum(jnp.where(eye, m, 0.0), axis=0, keepdims=True)
    s_row = jnp.sum(jnp.where(eye, esum, 0.0), axis=0, keepdims=True)
    upper = lax.broadcasted_iota(jnp.int32, (8, 128), 0) < 4
    stat_own[...] = jnp.where(upper, m_row, s_row)

    def stat_copy(do, peer):
        return pltpu.make_async_remote_copy(
            src_ref=stat_own,
            dst_ref=stat_all.at[NORIENT - do - 1],
            send_sem=st_send,
            recv_sem=st_recv,
            device_id=peer,
            device_id_type=MESH,
        )

    for do, peer in orient_peers:
        stat_copy(do, peer).start()

    def ag_slot(b, way, step):
        return sum(sum(h) for h in AG_HOPS[:b]) + (AG_HOPS[b][0] if way else 0) + step - 1

    def ag_copy(b, way, step):
        sign = 1 if way else -1
        c = lax.rem(z - sign * (step - 1) + NZ, NZ)
        return pltpu.make_async_remote_copy(
            src_ref=all_e.at[c, b],
            dst_ref=all_e.at[c, b],
            send_sem=ag_send,
            recv_sem=ag_recv.at[ag_slot(b, way, step)],
            device_id=at_z(sign),
            device_id_type=MESH,
        )

    def ag_step(step):
        for b in range(NB):
            for way in range(2):
                hops = AG_HOPS[b][way]
                if 1 <= step <= hops:
                    ag_copy(b, way, step).wait_recv()
                if step < hops:
                    ag_copy(b, way, step + 1).start()

    ag_step(0)
    ag_step(1)
    ag_step(2)

    pltpu.make_async_copy(stat_all, stat_all, st_recv).wait()
    big = m_row
    for j in range(NORIENT - 1):
        big = jnp.maximum(big, stat_all[j, 0:1, :])
    whole = s_row * jnp.exp(m_row - big)
    for j in range(NORIENT - 1):
        whole = whole + stat_all[j, 4:5, :] * jnp.exp(stat_all[j, 0:1, :] - big)
    lane = lax.broadcasted_iota(jnp.int32, (1, 128), 1)
    whole = jnp.where(lane < OWN, whole, 1.0)
    factor = jnp.exp(m_row - big) / whole
    fac_own[...] = jnp.broadcast_to(factor, (8, 128))

    def fac_copy(dz):
        return pltpu.make_async_remote_copy(
            src_ref=fac_own,
            dst_ref=fac_all.at[z],
            send_sem=fc_send,
            recv_sem=fc_recv,
            device_id=at_z(dz),
            device_id_type=MESH,
        )

    for dz in (4, 3, 5, 2, 6, 1, 7):
        fac_copy(dz).start()
    fac_all[z] = fac_own[...]

    ag_step(3)
    ag_step(4)
    fac_sent = fac_all.at[pl.ds(0, NZ - 1)]
    pltpu.make_async_copy(fac_sent, fac_sent, fc_recv).wait()

    cols = []
    for zz in range(NZ):
        f = jnp.sum(jnp.where(eye, fac_all[zz, 0:1, :], 0.0), axis=1, keepdims=True)
        cols.append(f)
    for b in range(NB):
        block = jnp.concatenate(
            [all_e[zz, b].astype(jnp.float32) * cols[zz] for zz in range(NZ)], axis=0
        )
        probs_ref[b * BS : (b + 1) * BS, :] = block.T.astype(jnp.bfloat16)

    pltpu.make_async_copy(recv, recv, rs_send).wait()
    pltpu.make_async_copy(y_out, y_out, y_send).wait()
    e_sent = all_e.at[pl.ds(0, NZ - 1)]
    pltpu.make_async_copy(e_sent, e_sent, ag_send).wait()
    pltpu.make_async_copy(stat_all, stat_all, st_send).wait()
    pltpu.make_async_copy(fac_sent, fac_sent, fc_send).wait()


NU = 8
UC = COLS // NU


def update_kernel(probs_ref, counts_ref, held_ref, out_ref, done, sem):
    norm = jnp.sum(probs_ref[...].astype(jnp.float32), axis=1, keepdims=True)
    inv = jnp.broadcast_to(1.0 / (norm + 1.0), (ROWS, 128))
    scale = jnp.concatenate([inv] * (UC // 128), axis=1)

    def put(u):
        return pltpu.make_async_copy(done.at[u], out_ref.at[:, pl.ds(u * UC, UC)], sem.at[u])

    for u in range(NU):
        k, c = divmod(u * UC, KC)
        num = jnp.dot(
            probs_ref[...], counts_ref[k, :, c : c + UC], preferred_element_type=jnp.float32
        )
        for b in range(NB):
            rows = slice(b * BS, (b + 1) * BS)
            x = held_ref[b, k, :, c : c + UC].astype(jnp.float32)
            done[u, rows, :] = ((num[rows] + x) * scale[rows]).astype(jnp.bfloat16)
        put(u).start()
    for u in range(NU):
        put(u).wait()


def on_device(model, patterns):
    f32, bf16 = jnp.float32, jnp.bfloat16
    dma = pltpu.SemaphoreType.DMA
    vmem = pl.BlockSpec(memory_space=pltpu.VMEM)
    hbm = pl.BlockSpec(memory_space=pltpu.HBM)
    rs_slots = sum(sum(h) for h in RS_HOPS)
    ag_slots = sum(sum(h) for h in AG_HOPS)
    probs, counts, held = pl.pallas_call(
        exchange_kernel,
        name="exchange",
        out_shape=(
            jax.ShapeDtypeStruct((ROWS, FRAMES), bf16),
            jax.ShapeDtypeStruct((NK, FRAMES, KC), bf16),
            jax.ShapeDtypeStruct((NB, NK, BS, KC), bf16),
        ),
        in_specs=[hbm] * 2,
        out_specs=(vmem,) * 3,
        scratch_shapes=[
            pltpu.VMEM((NK, FRAMES, KC), jnp.int32),
            pltpu.VMEM((NB, FRAMES, BS), f32),
            pltpu.VMEM((NB, BS, 128), f32),
            pltpu.VMEM((rs_slots, OWN, BS), f32),
            pltpu.VMEM((NB, OWN, BS), f32),
            pltpu.VMEM((NB, OWN, BS), f32),
            pltpu.VMEM((NZ, NB, OWN, BS), bf16),
            pltpu.VMEM((8, 128), f32),
            pltpu.VMEM((NORIENT - 1, 8, 128), f32),
            pltpu.VMEM((8, 128), f32),
            pltpu.VMEM((NZ, 8, 128), f32),
            dma((NK,)),
            dma((NB, NK)),
            dma,
            dma((rs_slots,)),
            dma,
            dma((NB,)),
            dma,
            dma((ag_slots,)),
            dma,
            dma,
            dma,
            dma,
        ],
        compiler_params=pltpu.CompilerParams(
            collective_id=0, has_side_effects=True, vmem_limit_bytes=40 * 1024 * 1024
        ),
    )(model, patterns)
    return pl.pallas_call(
        update_kernel,
        name="update",
        out_shape=jax.ShapeDtypeStruct((ROWS, COLS), bf16),
        in_specs=[vmem] * 3,
        out_specs=hbm,
        scratch_shapes=[pltpu.VMEM((NU, ROWS, UC), bf16), dma((NU,))],
        compiler_params=pltpu.CompilerParams(vmem_limit_bytes=30 * 1024 * 1024),
    )(probs, counts, held)


def solution(mesh):
    placed = (P("orient", "pix"), P(None, "pix"))
    return jax.shard_map(
        on_device, mesh=mesh, in_specs=placed, out_specs=P("orient", "pix"), check_vma=False
    )
```

```python
import math

import jax
import jax.numpy as jnp
from jax import lax
from jax.experimental import pallas as pl
from jax.experimental.pallas import tpu as pltpu
from jax.sharding import PartitionSpec as P

PIX = 65536
BETA = 2.0 / math.sqrt(PIX)
MESH = pl.DeviceIdType.MESH

ROWS = 768
COLS = 4096
FRAMES = 384
KC = 512
NK = COLS // KC
NB = 3
BS = ROWS // NB
NZ = 8
OWN = FRAMES // NZ
NORIENT = 16

RS_HOPS = ((4, 3), (3, 4), (4, 3))
AG_HOPS = ((4, 3), (3, 4), (4, 3))


def exchange_kernel(
    model_ref,
    pat_ref,
    probs_ref,
    cb,
    mv,
    pv,
    part,
    tot,
    recv,
    y_out,
    y_in,
    all_e,
    stat_own,
    stat_all,
    fac_own,
    fac_all,
    pat_sem,
    mod_sem,
    rs_send,
    rs_recv,
    y_send,
    y_recv,
    ag_send,
    ag_recv,
    st_send,
    st_recv,
    fc_send,
    fc_recv,
):
    o = lax.axis_index("orient")
    p = lax.axis_index("pix")
    y = p // NZ
    z = lax.rem(p, NZ)

    def at_z(dz):
        return (o, y * NZ + lax.rem(z + dz + NZ, NZ))

    y_peer = (o, (1 - y) * NZ + z)
    orient_peers = [(do, (lax.rem(o + do, NORIENT), p)) for do in range(1, NORIENT)]

    def pat_copy(k):
        return pltpu.make_async_copy(
            pat_ref.at[:, pl.ds(k * KC, KC)], pv.at[k], pat_sem.at[k]
        )

    def mod_copy(k):
        return pltpu.make_async_copy(
            model_ref.at[:, pl.ds(k * KC, KC)], mv.at[k], mod_sem.at[k]
        )

    for k in range(NK):
        pat_copy(k).start()
        mod_copy(k).start()

    barrier = pltpu.get_barrier_semaphore()
    for dz in range(1, NZ):
        pl.semaphore_signal(barrier, inc=1, device_id=at_z(dz), device_id_type=MESH)
    pl.semaphore_signal(barrier, inc=1, device_id=y_peer, device_id_type=MESH)
    for _, peer in orient_peers:
        pl.semaphore_signal(barrier, inc=1, device_id=peer, device_id_type=MESH)

    def own_part(b, c):
        row = pl.multiple_of(lax.rem(c + NZ, NZ) * OWN, 8)
        return part.at[b, pl.ds(row, OWN), :]

    def rs_slot(b, way, step):
        return sum(sum(h) for h in RS_HOPS[:b]) + (RS_HOPS[b][0] if way else 0) + step - 1

    def rs_copy(b, way, step):
        hops = RS_HOPS[b][way]
        sign = 1 if way else -1
        slot = rs_slot(b, way, step)
        left = hops - step + 1
        src = own_part(b, z + sign * left) if step == 1 else recv.at[slot - 1]
        return pltpu.make_async_remote_copy(
            src_ref=src,
            dst_ref=recv.at[slot],
            send_sem=rs_send,
            recv_sem=rs_recv.at[slot],
            device_id=at_z(sign),
            device_id_type=MESH,
        )

    def rs_start(b):
        for way in range(2):
            rs_copy(b, way, 1).start()

    def rs_step(b, step):
        for way in range(2):
            hops = RS_HOPS[b][way]
            if step > hops:
                continue
            rs_copy(b, way, step).wait_recv()
            if step < hops:
                sign = 1 if way else -1
                slot = rs_slot(b, way, step)
                recv[slot] += own_part(b, z + sign * (hops - step))[...]
                rs_copy(b, way, step + 1).start()

    def y_copy(b):
        return pltpu.make_async_remote_copy(
            src_ref=y_out.at[b],
            dst_ref=y_in.at[b],
            send_sem=y_send,
            recv_sem=y_recv.at[b],
            device_id=y_peer,
            device_id_type=MESH,
        )

    def rs_end(b):
        low = recv[rs_slot(b, 0, RS_HOPS[b][0])]
        high = recv[rs_slot(b, 1, RS_HOPS[b][1])]
        y_out[b] = own_part(b, z)[...] + (low + high)
        y_copy(b).start()

    ones = jnp.ones((8, 128), jnp.float32)

    def chunk(k, carry):
        mod_copy(k).wait()
        pat_copy(k).wait()
        c = pv[k].astype(jnp.float32).astype(jnp.bfloat16)
        cb[k] = c
        x = mv[k].astype(jnp.float32)
        t = tot[...]
        for j in range(KC // 128):
            t = t + x[:, j * 128 : (j + 1) * 128]
        tot[...] = t
        logs = jnp.log(x)
        hi = logs.astype(jnp.bfloat16)
        lo = (logs - hi.astype(jnp.float32)).astype(jnp.bfloat16)
        twice = jnp.concatenate([c, c], axis=1)
        for b in range(NB):
            rows = slice(b * BS, (b + 1) * BS)
            part[b] += lax.dot_general(
                twice,
                jnp.concatenate([hi[rows], lo[rows]], axis=1),
                (((1,), (1,)), ((), ())),
                preferred_element_type=jnp.float32,
            )
        return carry

    def finish(b):
        row = lax.dot_general(
            ones,
            tot[b * BS : (b + 1) * BS],
            (((1,), (1,)), ((), ())),
            precision=lax.Precision.HIGHEST,
            preferred_element_type=jnp.float32,
        )
        part[b] -= row[0:1, :]

    tail = [("step", b, step) for step in range(1, 5) for b in range(NB)]
    tail = tail[:-2] + [("end", 0)] + tail[-2:-1] + [("end", 1)] + tail[-1:] + [("end", 2)]

    def act(hook):
        kind, b = hook[0], hook[1]
        if kind == "start":
            if b == 0:
                pl.semaphore_wait(barrier, NZ + len(orient_peers))
            rs_start(b)
        elif kind == "step":
            rs_step(b, hook[2])
        else:
            rs_end(b)

    tot[...] = jnp.zeros_like(tot)
    part[...] = jnp.zeros_like(part)
    lax.fori_loop(0, NK, chunk, 0)
    for b in range(NB):
        finish(b)
        act(("start", b))
    for hook in tail:
        act(hook)

    scores = []
    for b in range(NB):
        y_copy(b).wait_recv()
        scores.append(BETA * (y_out[b] + y_in[b]))

    m = jnp.max(jnp.maximum(jnp.maximum(scores[0], scores[1]), scores[2]), axis=1, keepdims=True)
    acc = jnp.zeros((OWN, BS), jnp.float32)
    for b in range(NB):
        e = jnp.exp(scores[b] - m)
        acc = acc + e
        all_e[z, b] = e.astype(jnp.bfloat16)
    esum = jnp.sum(acc, axis=1, keepdims=True)
    eye = lax.broadcasted_iota(jnp.int32, (OWN, 128), 0) == lax.broadcasted_iota(
        jnp.int32, (OWN, 128), 1
    )
    m_row = jnp.sum(jnp.where(eye, m, 0.0), axis=0, keepdims=True)
    s_row = jnp.sum(jnp.where(eye, esum, 0.0), axis=0, keepdims=True)
    upper = lax.broadcasted_iota(jnp.int32, (8, 128), 0) < 4
    stat_own[...] = jnp.where(upper, m_row, s_row)

    def stat_copy(do, peer):
        return pltpu.make_async_remote_copy(
            src_ref=stat_own,
            dst_ref=stat_all.at[NORIENT - do - 1],
            send_sem=st_send,
            recv_sem=st_recv,
            device_id=peer,
            device_id_type=MESH,
        )

    for do, peer in orient_peers:
        stat_copy(do, peer).start()

    def ag_slot(b, way, step):
        return sum(sum(h) for h in AG_HOPS[:b]) + (AG_HOPS[b][0] if way else 0) + step - 1

    def ag_copy(b, way, step):
        sign = 1 if way else -1
        c = lax.rem(z - sign * (step - 1) + NZ, NZ)
        return pltpu.make_async_remote_copy(
            src_ref=all_e.at[c, b],
            dst_ref=all_e.at[c, b],
            send_sem=ag_send,
            recv_sem=ag_recv.at[ag_slot(b, way, step)],
            device_id=at_z(sign),
            device_id_type=MESH,
        )

    def ag_step(step):
        for b in range(NB):
            for way in range(2):
                hops = AG_HOPS[b][way]
                if 1 <= step <= hops:
                    ag_copy(b, way, step).wait_recv()
                if step < hops:
                    ag_copy(b, way, step + 1).start()

    ag_step(0)
    ag_step(1)
    ag_step(2)

    pltpu.make_async_copy(stat_all, stat_all, st_recv).wait()
    big = m_row
    for j in range(NORIENT - 1):
        big = jnp.maximum(big, stat_all[j, 0:1, :])
    whole = s_row * jnp.exp(m_row - big)
    for j in range(NORIENT - 1):
        whole = whole + stat_all[j, 4:5, :] * jnp.exp(stat_all[j, 0:1, :] - big)
    lane = lax.broadcasted_iota(jnp.int32, (1, 128), 1)
    whole = jnp.where(lane < OWN, whole, 1.0)
    factor = jnp.exp(m_row - big) / whole
    fac_own[...] = jnp.broadcast_to(factor, (8, 128))

    def fac_copy(dz):
        return pltpu.make_async_remote_copy(
            src_ref=fac_own,
            dst_ref=fac_all.at[z],
            send_sem=fc_send,
            recv_sem=fc_recv,
            device_id=at_z(dz),
            device_id_type=MESH,
        )

    for dz in (4, 3, 5, 2, 6, 1, 7):
        fac_copy(dz).start()
    fac_all[z] = fac_own[...]

    ag_step(3)
    ag_step(4)
    fac_sent = fac_all.at[pl.ds(0, NZ - 1)]
    pltpu.make_async_copy(fac_sent, fac_sent, fc_recv).wait()

    cols = []
    for zz in range(NZ):
        f = jnp.sum(jnp.where(eye, fac_all[zz, 0:1, :], 0.0), axis=1, keepdims=True)
        cols.append(f)
    for b in range(NB):
        block = jnp.concatenate(
            [all_e[zz, b].astype(jnp.float32) * cols[zz] for zz in range(NZ)], axis=0
        )
        probs_ref[b * BS : (b + 1) * BS, :] = block.T.astype(jnp.bfloat16)

    pltpu.make_async_copy(recv, recv, rs_send).wait()
    pltpu.make_async_copy(y_out, y_out, y_send).wait()
    e_sent = all_e.at[pl.ds(0, NZ - 1)]
    pltpu.make_async_copy(e_sent, e_sent, ag_send).wait()
    pltpu.make_async_copy(stat_all, stat_all, st_send).wait()
    pltpu.make_async_copy(fac_sent, fac_sent, fc_send).wait()


NU = 8
UC = COLS // NU


def update_kernel(probs_ref, counts_ref, held_ref, out_ref, done, sem):
    norm = jnp.sum(probs_ref[...].astype(jnp.float32), axis=1, keepdims=True)
    inv = jnp.broadcast_to(1.0 / (norm + 1.0), (ROWS, 128))
    scale = jnp.concatenate([inv] * (UC // 128), axis=1)

    def put(u):
        return pltpu.make_async_copy(done.at[u], out_ref.at[:, pl.ds(u * UC, UC)], sem.at[u])

    for u in range(NU):
        k, c = divmod(u * UC, KC)
        num = jnp.dot(
            probs_ref[...], counts_ref[k, :, c : c + UC], preferred_element_type=jnp.float32
        )
        for b in range(NB):
            rows = slice(b * BS, (b + 1) * BS)
            x = held_ref[k, rows, c : c + UC].astype(jnp.float32)
            done[u, rows, :] = ((num[rows] + x) * scale[rows]).astype(jnp.bfloat16)
        put(u).start()
    for u in range(NU):
        put(u).wait()


def on_device(model, patterns):
    f32, bf16 = jnp.float32, jnp.bfloat16
    dma = pltpu.SemaphoreType.DMA
    vmem = pl.BlockSpec(memory_space=pltpu.VMEM)
    hbm = pl.BlockSpec(memory_space=pltpu.HBM)
    rs_slots = sum(sum(h) for h in RS_HOPS)
    ag_slots = sum(sum(h) for h in AG_HOPS)
    probs, counts, held = pl.pallas_call(
        exchange_kernel,
        name="exchange",
        out_shape=(
            jax.ShapeDtypeStruct((ROWS, FRAMES), bf16),
            jax.ShapeDtypeStruct((NK, FRAMES, KC), bf16),
            jax.ShapeDtypeStruct((NK, ROWS, KC), bf16),
        ),
        in_specs=[hbm] * 2,
        out_specs=(vmem,) * 3,
        scratch_shapes=[
            pltpu.VMEM((NK, FRAMES, KC), jnp.int32),
            pltpu.VMEM((NB, FRAMES, BS), f32),
            pltpu.VMEM((ROWS, 128), f32),
            pltpu.VMEM((rs_slots, OWN, BS), f32),
            pltpu.VMEM((NB, OWN, BS), f32),
            pltpu.VMEM((NB, OWN, BS), f32),
            pltpu.VMEM((NZ, NB, OWN, BS), bf16),
            pltpu.VMEM((8, 128), f32),
            pltpu.VMEM((NORIENT - 1, 8, 128), f32),
            pltpu.VMEM((8, 128), f32),
            pltpu.VMEM((NZ, 8, 128), f32),
            dma((NK,)),
            dma((NK,)),
            dma,
            dma((rs_slots,)),
            dma,
            dma((NB,)),
            dma,
            dma((ag_slots,)),
            dma,
            dma,
            dma,
            dma,
        ],
        compiler_params=pltpu.CompilerParams(
            collective_id=0, has_side_effects=True, vmem_limit_bytes=40 * 1024 * 1024
        ),
    )(model, patterns)
    return pl.pallas_call(
        update_kernel,
        name="update",
        out_shape=jax.ShapeDtypeStruct((ROWS, COLS), bf16),
        in_specs=[vmem] * 3,
        out_specs=hbm,
        scratch_shapes=[pltpu.VMEM((NU, ROWS, UC), bf16), dma((NU,))],
        compiler_params=pltpu.CompilerParams(vmem_limit_bytes=30 * 1024 * 1024),
    )(probs, counts, held)


def solution(mesh):
    placed = (P("orient", "pix"), P(None, "pix"))
    return jax.shard_map(
        on_device, mesh=mesh, in_specs=placed, out_specs=P("orient", "pix"), check_vma=False
    )
```

```python
import math

import jax
import jax.numpy as jnp
from jax import lax
from jax.experimental import pallas as pl
from jax.experimental.pallas import tpu as pltpu
from jax.sharding import PartitionSpec as P

PIX = 65536
BETA = 2.0 / math.sqrt(PIX)
MESH = pl.DeviceIdType.MESH

ROWS = 768
COLS = 4096
FRAMES = 384
KC = 512
NK = COLS // KC
NB = 3
BS = ROWS // NB
NZ = 8
OWN = FRAMES // NZ
NORIENT = 16

RS_HOPS = ((4, 3), (3, 4), (4, 3))


def exchange_kernel(
    model_ref,
    pat_ref,
    probs_ref,
    cb,
    mv,
    pv,
    part,
    tot,
    recv,
    y_out,
    y_in,
    all_e,
    stat_own,
    stat_all,
    fac_own,
    fac_all,
    turned,
    pat_sem,
    mod_sem,
    rs_send,
    rs_recv,
    y_send,
    y_recv,
    ag_send,
    ag_recv,
    st_send,
    st_recv,
    fc_send,
    fc_recv,
):
    o = lax.axis_index("orient")
    p = lax.axis_index("pix")
    y = p // NZ
    z = lax.rem(p, NZ)

    def at_z(dz):
        return (o, y * NZ + lax.rem(z + dz + NZ, NZ))

    y_peer = (o, (1 - y) * NZ + z)
    orient_peers = [(do, (lax.rem(o + do, NORIENT), p)) for do in range(1, NORIENT)]

    def pat_copy(k):
        return pltpu.make_async_copy(
            pat_ref.at[:, pl.ds(k * KC, KC)], pv.at[k], pat_sem.at[k]
        )

    def mod_copy(k):
        return pltpu.make_async_copy(
            model_ref.at[:, pl.ds(k * KC, KC)], mv.at[k], mod_sem.at[k]
        )

    for k in range(NK):
        pat_copy(k).start()
        mod_copy(k).start()

    barrier = pltpu.get_barrier_semaphore()
    for dz in range(1, NZ):
        pl.semaphore_signal(barrier, inc=1, device_id=at_z(dz), device_id_type=MESH)
    pl.semaphore_signal(barrier, inc=1, device_id=y_peer, device_id_type=MESH)
    for _, peer in orient_peers:
        pl.semaphore_signal(barrier, inc=1, device_id=peer, device_id_type=MESH)

    def own_part(b, c):
        row = pl.multiple_of(lax.rem(c + NZ, NZ) * OWN, 8)
        return part.at[b, pl.ds(row, OWN), :]

    def rs_slot(b, way, step):
        return sum(sum(h) for h in RS_HOPS[:b]) + (RS_HOPS[b][0] if way else 0) + step - 1

    def rs_copy(b, way, step):
        hops = RS_HOPS[b][way]
        sign = 1 if way else -1
        slot = rs_slot(b, way, step)
        left = hops - step + 1
        src = own_part(b, z + sign * left) if step == 1 else recv.at[slot - 1]
        return pltpu.make_async_remote_copy(
            src_ref=src,
            dst_ref=recv.at[slot],
            send_sem=rs_send,
            recv_sem=rs_recv.at[slot],
            device_id=at_z(sign),
            device_id_type=MESH,
        )

    def rs_start(b):
        for way in range(2):
            rs_copy(b, way, 1).start()

    def rs_step(b, step):
        for way in range(2):
            hops = RS_HOPS[b][way]
            if step > hops:
                continue
            rs_copy(b, way, step).wait_recv()
            if step < hops:
                sign = 1 if way else -1
                slot = rs_slot(b, way, step)
                recv[slot] += own_part(b, z + sign * (hops - step))[...]
                rs_copy(b, way, step + 1).start()

    def y_copy(b):
        return pltpu.make_async_remote_copy(
            src_ref=y_out.at[b],
            dst_ref=y_in.at[b],
            send_sem=y_send,
            recv_sem=y_recv.at[b],
            device_id=y_peer,
            device_id_type=MESH,
        )

    def rs_end(b):
        low = recv[rs_slot(b, 0, RS_HOPS[b][0])]
        high = recv[rs_slot(b, 1, RS_HOPS[b][1])]
        y_out[b] = own_part(b, z)[...] + (low + high)
        y_copy(b).start()

    ones = jnp.ones((8, 128), jnp.float32)

    def chunk(k, carry):
        mod_copy(k).wait()
        pat_copy(k).wait()
        c = pv[k].astype(jnp.float32).astype(jnp.bfloat16)
        cb[k] = c
        x = mv[k].astype(jnp.float32)
        t = tot[...]
        for j in range(KC // 128):
            t = t + x[:, j * 128 : (j + 1) * 128]
        tot[...] = t
        logs = jnp.log(x)
        hi = logs.astype(jnp.bfloat16)
        lo = (logs - hi.astype(jnp.float32)).astype(jnp.bfloat16)
        twice = jnp.concatenate([c, c], axis=1)
        for b in range(NB):
            rows = slice(b * BS, (b + 1) * BS)
            part[b] += lax.dot_general(
                twice,
                jnp.concatenate([hi[rows], lo[rows]], axis=1),
                (((1,), (1,)), ((), ())),
                preferred_element_type=jnp.float32,
            )
        return carry

    def finish():
        row = lax.dot_general(
            ones,
            tot[...],
            (((1,), (1,)), ((), ())),
            precision=lax.Precision.HIGHEST,
            preferred_element_type=jnp.float32,
        )
        for b in range(NB):
            part[b] -= row[0:1, b * BS : (b + 1) * BS]
            act(("start", b))

    tail = [("step", b, step) for step in range(1, 5) for b in range(NB)]
    tail = tail[:-2] + [("end", 0)] + tail[-2:-1] + [("end", 1)] + tail[-1:] + [("end", 2)]

    def act(hook):
        kind, b = hook[0], hook[1]
        if kind == "start":
            if b == 0:
                pl.semaphore_wait(barrier, NZ + len(orient_peers))
            rs_start(b)
        elif kind == "step":
            rs_step(b, hook[2])
        else:
            rs_end(b)

    tot[...] = jnp.zeros_like(tot)
    part[...] = jnp.zeros_like(part)
    lax.fori_loop(0, NK, chunk, 0)
    finish()
    for hook in tail:
        act(hook)

    def ag_copy(b, dz):
        return pltpu.make_async_remote_copy(
            src_ref=all_e.at[z, b],
            dst_ref=all_e.at[z, b],
            send_sem=ag_send,
            recv_sem=ag_recv,
            device_id=at_z(dz),
            device_id_type=MESH,
        )

    scores = []
    for b in range(NB):
        y_copy(b).wait_recv()
        scores.append(BETA * (y_out[b] + y_in[b]))
    m = jnp.max(jnp.maximum(jnp.maximum(scores[0], scores[1]), scores[2]), axis=1, keepdims=True)
    acc = jnp.zeros((OWN, BS), jnp.float32)
    for b in range(NB):
        e = jnp.exp(scores[b] - m)
        acc = acc + e
        all_e[z, b] = e.astype(jnp.bfloat16)
    esum = jnp.sum(acc, axis=1, keepdims=True)
    row = lax.broadcasted_iota(jnp.int32, (OWN, 128), 0)
    lane = lax.broadcasted_iota(jnp.int32, (OWN, 128), 1)
    stat_own[...] = jnp.sum(
        jnp.where(lane == row, m, jnp.where(lane == row + 64, esum, 0.0)), axis=0, keepdims=True
    )

    def stat_copy(do, peer):
        return pltpu.make_async_remote_copy(
            src_ref=stat_own,
            dst_ref=stat_all.at[NORIENT - do - 1],
            send_sem=st_send,
            recv_sem=st_recv,
            device_id=peer,
            device_id_type=MESH,
        )

    for do, peer in orient_peers:
        stat_copy(do, peer).start()
    for b in range(NB):
        for dz in (4, 3, 5, 2, 6, 1, 7):
            ag_copy(b, dz).start()

    stat_all[NORIENT - 1] = stat_own[...]
    stats_sent = stat_all.at[pl.ds(0, NORIENT - 1)]
    pltpu.make_async_copy(stats_sent, stats_sent, st_recv).wait()
    stats = stat_all[:, 0, :]
    big = jnp.max(stats, axis=0, keepdims=True)
    weight = jnp.exp(stats - big)
    whole = jnp.sum(pltpu.roll(stats, 64, 1) * weight, axis=0, keepdims=True)
    used = lax.broadcasted_iota(jnp.int32, (1, 128), 1) < OWN
    fac_own[...] = jnp.where(used, jnp.exp(stat_own[...] - big) / jnp.where(used, whole, 1.0), 0.0)

    def fac_copy(dz):
        return pltpu.make_async_remote_copy(
            src_ref=fac_own,
            dst_ref=fac_all.at[z],
            send_sem=fc_send,
            recv_sem=fc_recv,
            device_id=at_z(dz),
            device_id_type=MESH,
        )

    for dz in (4, 3, 5, 2, 6, 1, 7):
        fac_copy(dz).start()
    fac_all[z] = fac_own[...]

    e_sent = all_e.at[pl.ds(0, NZ - 1)]
    fac_sent = fac_all.at[pl.ds(0, NZ - 1)]
    pltpu.make_async_copy(e_sent, e_sent, ag_recv).wait()
    for b in range(NB):
        block = jnp.concatenate([all_e[zz, b].astype(jnp.float32) for zz in range(NZ)], axis=0)
        turned[b * BS : (b + 1) * BS, :] = block.T

    pltpu.make_async_copy(fac_sent, fac_sent, fc_recv).wait()
    pad = jnp.zeros((1, FRAMES - 128), jnp.float32)
    factors = jnp.zeros((1, FRAMES), jnp.float32)
    for zz in range(NZ):
        piece = jnp.concatenate([fac_all[zz], pad], axis=1)
        factors = factors + (pltpu.roll(piece, zz * OWN, 1) if zz else piece)
    for b in range(NB):
        rows = slice(b * BS, (b + 1) * BS)
        probs_ref[rows, :] = (turned[rows, :] * factors).astype(jnp.bfloat16)

    pltpu.make_async_copy(recv, recv, rs_send).wait()
    pltpu.make_async_copy(y_out, y_out, y_send).wait()
    pltpu.make_async_copy(e_sent, e_sent, ag_send).wait()
    pltpu.make_async_copy(stats_sent, stats_sent, st_send).wait()
    pltpu.make_async_copy(fac_sent, fac_sent, fc_send).wait()


NU = 8
UC = COLS // NU


def update_kernel(probs_ref, counts_ref, held_ref, out_ref, done, sem):
    norm = jnp.sum(probs_ref[...].astype(jnp.float32), axis=1, keepdims=True)
    inv = jnp.broadcast_to(1.0 / (norm + 1.0), (ROWS, 128))
    scale = jnp.concatenate([inv] * (UC // 128), axis=1)

    def put(u):
        return pltpu.make_async_copy(done.at[u], out_ref.at[:, pl.ds(u * UC, UC)], sem.at[u])

    for u in range(NU):
        k, c = divmod(u * UC, KC)
        num = jnp.dot(
            probs_ref[...], counts_ref[k, :, c : c + UC], preferred_element_type=jnp.float32
        )
        for b in range(NB):
            rows = slice(b * BS, (b + 1) * BS)
            x = held_ref[k, rows, c : c + UC].astype(jnp.float32)
            done[u, rows, :] = ((num[rows] + x) * scale[rows]).astype(jnp.bfloat16)
        put(u).start()
    for u in range(NU):
        put(u).wait()


def on_device(model, patterns):
    f32, bf16 = jnp.float32, jnp.bfloat16
    dma = pltpu.SemaphoreType.DMA
    vmem = pl.BlockSpec(memory_space=pltpu.VMEM)
    hbm = pl.BlockSpec(memory_space=pltpu.HBM)
    rs_slots = sum(sum(h) for h in RS_HOPS)
    probs, counts, held = pl.pallas_call(
        exchange_kernel,
        name="exchange",
        out_shape=(
            jax.ShapeDtypeStruct((ROWS, FRAMES), bf16),
            jax.ShapeDtypeStruct((NK, FRAMES, KC), bf16),
            jax.ShapeDtypeStruct((NK, ROWS, KC), bf16),
        ),
        in_specs=[hbm] * 2,
        out_specs=(vmem,) * 3,
        scratch_shapes=[
            pltpu.VMEM((NK, FRAMES, KC), jnp.int32),
            pltpu.VMEM((NB, FRAMES, BS), f32),
            pltpu.VMEM((ROWS, 128), f32),
            pltpu.VMEM((rs_slots, OWN, BS), f32),
            pltpu.VMEM((NB, OWN, BS), f32),
            pltpu.VMEM((NB, OWN, BS), f32),
            pltpu.VMEM((NZ, NB, OWN, BS), bf16),
            pltpu.VMEM((1, 128), f32),
            pltpu.VMEM((NORIENT, 1, 128), f32),
            pltpu.VMEM((1, 128), f32),
            pltpu.VMEM((NZ, 1, 128), f32),
            pltpu.VMEM((ROWS, FRAMES), f32),
            dma((NK,)),
            dma((NK,)),
            dma,
            dma((rs_slots,)),
            dma,
            dma((NB,)),
            dma,
            dma,
            dma,
            dma,
            dma,
            dma,
        ],
        compiler_params=pltpu.CompilerParams(
            collective_id=0, has_side_effects=True, vmem_limit_bytes=40 * 1024 * 1024
        ),
    )(model, patterns)
    return pl.pallas_call(
        update_kernel,
        name="update",
        out_shape=jax.ShapeDtypeStruct((ROWS, COLS), bf16),
        in_specs=[vmem] * 3,
        out_specs=hbm,
        scratch_shapes=[pltpu.VMEM((NU, ROWS, UC), bf16), dma((NU,))],
        compiler_params=pltpu.CompilerParams(vmem_limit_bytes=30 * 1024 * 1024),
    )(probs, counts, held)


def solution(mesh):
    placed = (P("orient", "pix"), P(None, "pix"))
    return jax.shard_map(
        on_device, mesh=mesh, in_specs=placed, out_specs=P("orient", "pix"), check_vma=False
    )
```

```python
import math

import jax
import jax.numpy as jnp
from jax import lax
from jax.experimental import pallas as pl
from jax.experimental.pallas import tpu as pltpu
from jax.sharding import PartitionSpec as P

PIX = 65536
BETA = 2.0 / math.sqrt(PIX)
MESH = pl.DeviceIdType.MESH

ROWS = 768
COLS = 4096
FRAMES = 384
KC = 512
NK = COLS // KC
NB = 3
BS = ROWS // NB
NZ = 8
OWN = FRAMES // NZ
NORIENT = 16

RS_HOPS = (((4, 3), (3, 4)) * 3)[:3]


def exchange_kernel(
    model_ref,
    pat_ref,
    probs_ref,
    cb,
    mv,
    pv,
    part,
    tot,
    recv,
    y_out,
    y_in,
    all_e,
    stat_own,
    stat_all,
    fac_own,
    fac_all,
    turned,
    pat_sem,
    mod_sem,
    rs_send,
    rs_recv,
    y_send,
    y_recv,
    ag_send,
    ag_recv,
    st_send,
    st_recv,
    fc_send,
    fc_recv,
):
    o = lax.axis_index("orient")
    p = lax.axis_index("pix")
    y = p // NZ
    z = lax.rem(p, NZ)

    def at_z(dz):
        return (o, y * NZ + lax.rem(z + dz + NZ, NZ))

    y_peer = (o, (1 - y) * NZ + z)
    orient_peers = [(do, (lax.rem(o + do, NORIENT), p)) for do in range(1, NORIENT)]

    def pat_copy(k):
        return pltpu.make_async_copy(
            pat_ref.at[:, pl.ds(k * KC, KC)], pv.at[k], pat_sem.at[k]
        )

    def mod_copy(k):
        return pltpu.make_async_copy(
            model_ref.at[:, pl.ds(k * KC, KC)], mv.at[k], mod_sem.at[k]
        )

    for k in range(NK):
        pat_copy(k).start()
        mod_copy(k).start()

    barrier = pltpu.get_barrier_semaphore()
    for dz in range(1, NZ):
        pl.semaphore_signal(barrier, inc=1, device_id=at_z(dz), device_id_type=MESH)
    pl.semaphore_signal(barrier, inc=1, device_id=y_peer, device_id_type=MESH)
    for _, peer in orient_peers:
        pl.semaphore_signal(barrier, inc=1, device_id=peer, device_id_type=MESH)

    def own_part(b, c):
        row = pl.multiple_of(lax.rem(c + NZ, NZ) * OWN, 8)
        return part.at[b, pl.ds(row, OWN), :]

    def rs_slot(b, way, step):
        return sum(sum(h) for h in RS_HOPS[:b]) + (RS_HOPS[b][0] if way else 0) + step - 1

    def rs_copy(b, way, step):
        hops = RS_HOPS[b][way]
        sign = 1 if way else -1
        slot = rs_slot(b, way, step)
        left = hops - step + 1
        src = own_part(b, z + sign * left) if step == 1 else recv.at[slot - 1]
        return pltpu.make_async_remote_copy(
            src_ref=src,
            dst_ref=recv.at[slot],
            send_sem=rs_send,
            recv_sem=rs_recv.at[slot],
            device_id=at_z(sign),
            device_id_type=MESH,
        )

    def rs_start(b):
        for way in range(2):
            rs_copy(b, way, 1).start()

    def rs_step(b, step):
        for way in range(2):
            hops = RS_HOPS[b][way]
            if step > hops:
                continue
            rs_copy(b, way, step).wait_recv()
            if step < hops:
                sign = 1 if way else -1
                slot = rs_slot(b, way, step)
                recv[slot] += own_part(b, z + sign * (hops - step))[...]
                rs_copy(b, way, step + 1).start()

    def y_copy(b):
        return pltpu.make_async_remote_copy(
            src_ref=y_out.at[b],
            dst_ref=y_in.at[b],
            send_sem=y_send,
            recv_sem=y_recv.at[b],
            device_id=y_peer,
            device_id_type=MESH,
        )

    def rs_end(b):
        low = recv[rs_slot(b, 0, RS_HOPS[b][0])]
        high = recv[rs_slot(b, 1, RS_HOPS[b][1])]
        y_out[b] = own_part(b, z)[...] + (low + high)
        y_copy(b).start()

    ones = jnp.ones((8, 128), jnp.float32)

    def chunk(k, carry):
        mod_copy(k).wait()
        pat_copy(k).wait()
        c = pv[k].astype(jnp.float32).astype(jnp.bfloat16)
        cb[k] = c
        x = mv[k].astype(jnp.float32)
        t = tot[...]
        for j in range(KC // 128):
            t = t + x[:, j * 128 : (j + 1) * 128]
        tot[...] = t
        logs = jnp.log(x)
        hi = logs.astype(jnp.bfloat16)
        lo = (logs - hi.astype(jnp.float32)).astype(jnp.bfloat16)
        twice = jnp.concatenate([c, c], axis=1)
        d = lax.dot_general(
            twice,
            jnp.concatenate([hi, lo], axis=1),
            (((1,), (1,)), ((), ())),
            preferred_element_type=jnp.float32,
        )
        for b in range(NB):
            part[b] += d[:, b * BS : (b + 1) * BS]
        return carry

    def finish():
        row = lax.dot_general(
            ones,
            tot[...],
            (((1,), (1,)), ((), ())),
            precision=lax.Precision.HIGHEST,
            preferred_element_type=jnp.float32,
        )
        for b in range(NB):
            part[b] -= row[0:1, b * BS : (b + 1) * BS]
            act(("start", b))

    tail = [("step", b, step) for step in range(1, 4) for b in range(NB)]
    for b in range(NB):
        tail += [("step", b, 4), ("end", b)]

    def act(hook):
        kind, b = hook[0], hook[1]
        if kind == "start":
            if b == 0:
                pl.semaphore_wait(barrier, NZ + len(orient_peers))
            rs_start(b)
        elif kind == "step":
            rs_step(b, hook[2])
        else:
            rs_end(b)

    tot[...] = jnp.zeros_like(tot)
    part[...] = jnp.zeros_like(part)
    lax.fori_loop(0, NK, chunk, 0)
    finish()
    for hook in tail:
        act(hook)

    def ag_copy(b, dz):
        return pltpu.make_async_remote_copy(
            src_ref=all_e.at[z, b],
            dst_ref=all_e.at[z, b],
            send_sem=ag_send,
            recv_sem=ag_recv,
            device_id=at_z(dz),
            device_id_type=MESH,
        )

    scores = []
    for b in range(NB):
        y_copy(b).wait_recv()
        scores.append(BETA * (y_out[b] + y_in[b]))
    top = scores[0]
    for b in range(1, NB):
        top = jnp.maximum(top, scores[b])
    m = jnp.max(top, axis=1, keepdims=True)
    acc = jnp.zeros((OWN, BS), jnp.float32)
    for b in range(NB):
        e = jnp.exp(scores[b] - m)
        acc = acc + e
        all_e[z, b] = e.astype(jnp.bfloat16)
    esum = jnp.sum(acc, axis=1, keepdims=True)
    row = lax.broadcasted_iota(jnp.int32, (OWN, 128), 0)
    lane = lax.broadcasted_iota(jnp.int32, (OWN, 128), 1)
    stat_own[...] = jnp.sum(
        jnp.where(lane == row, m, jnp.where(lane == row + 64, esum, 0.0)), axis=0, keepdims=True
    )

    def stat_copy(do, peer):
        return pltpu.make_async_remote_copy(
            src_ref=stat_own,
            dst_ref=stat_all.at[NORIENT - do - 1],
            send_sem=st_send,
            recv_sem=st_recv,
            device_id=peer,
            device_id_type=MESH,
        )

    for do, peer in orient_peers:
        stat_copy(do, peer).start()
    for b in range(NB):
        for dz in (4, 3, 5, 2, 6, 1, 7):
            ag_copy(b, dz).start()

    stat_all[NORIENT - 1] = stat_own[...]
    stats_sent = stat_all.at[pl.ds(0, NORIENT - 1)]
    pltpu.make_async_copy(stats_sent, stats_sent, st_recv).wait()
    stats = stat_all[:, 0, :]
    big = jnp.max(stats, axis=0, keepdims=True)
    weight = jnp.exp(stats - big)
    whole = jnp.sum(pltpu.roll(stats, 64, 1) * weight, axis=0, keepdims=True)
    used = lax.broadcasted_iota(jnp.int32, (1, 128), 1) < OWN
    fac_own[...] = jnp.where(used, jnp.exp(stat_own[...] - big) / jnp.where(used, whole, 1.0), 0.0)

    def fac_copy(dz):
        return pltpu.make_async_remote_copy(
            src_ref=fac_own,
            dst_ref=fac_all.at[z],
            send_sem=fc_send,
            recv_sem=fc_recv,
            device_id=at_z(dz),
            device_id_type=MESH,
        )

    for dz in (4, 3, 5, 2, 6, 1, 7):
        fac_copy(dz).start()
    fac_all[z] = fac_own[...]

    e_sent = all_e.at[pl.ds(0, NZ - 1)]
    fac_sent = fac_all.at[pl.ds(0, NZ - 1)]
    pltpu.make_async_copy(e_sent, e_sent, ag_recv).wait()
    for b in range(NB):
        block = jnp.concatenate([all_e[zz, b].astype(jnp.float32) for zz in range(NZ)], axis=0)
        turned[b * BS : (b + 1) * BS, :] = block.T

    pltpu.make_async_copy(fac_sent, fac_sent, fc_recv).wait()
    pad = jnp.zeros((1, FRAMES - 128), jnp.float32)
    factors = jnp.zeros((1, FRAMES), jnp.float32)
    for zz in range(NZ):
        piece = jnp.concatenate([fac_all[zz], pad], axis=1)
        factors = factors + (pltpu.roll(piece, zz * OWN, 1) if zz else piece)
    for b in range(NB):
        rows = slice(b * BS, (b + 1) * BS)
        probs_ref[rows, :] = (turned[rows, :] * factors).astype(jnp.bfloat16)

    pltpu.make_async_copy(recv, recv, rs_send).wait()
    pltpu.make_async_copy(y_out, y_out, y_send).wait()
    pltpu.make_async_copy(e_sent, e_sent, ag_send).wait()
    pltpu.make_async_copy(stats_sent, stats_sent, st_send).wait()
    pltpu.make_async_copy(fac_sent, fac_sent, fc_send).wait()


NU = 8
UC = COLS // NU


def update_kernel(probs_ref, counts_ref, held_ref, out_ref, done, sem):
    norm = jnp.sum(probs_ref[...].astype(jnp.float32), axis=1, keepdims=True)
    inv = jnp.broadcast_to(1.0 / (norm + 1.0), (ROWS, 128))
    scale = jnp.concatenate([inv] * (UC // 128), axis=1)

    def put(u):
        return pltpu.make_async_copy(done.at[u], out_ref.at[:, pl.ds(u * UC, UC)], sem.at[u])

    for u in range(NU):
        k, c = divmod(u * UC, KC)
        num = jnp.dot(
            probs_ref[...], counts_ref[k, :, c : c + UC], preferred_element_type=jnp.float32
        )
        for b in range(NB):
            rows = slice(b * BS, (b + 1) * BS)
            x = held_ref[k, rows, c : c + UC].astype(jnp.float32)
            done[u, rows, :] = ((num[rows] + x) * scale[rows]).astype(jnp.bfloat16)
        put(u).start()
    for u in range(NU):
        put(u).wait()


def on_device(model, patterns):
    f32, bf16 = jnp.float32, jnp.bfloat16
    dma = pltpu.SemaphoreType.DMA
    vmem = pl.BlockSpec(memory_space=pltpu.VMEM)
    hbm = pl.BlockSpec(memory_space=pltpu.HBM)
    rs_slots = sum(sum(h) for h in RS_HOPS)
    probs, counts, held = pl.pallas_call(
        exchange_kernel,
        name="exchange",
        out_shape=(
            jax.ShapeDtypeStruct((ROWS, FRAMES), bf16),
            jax.ShapeDtypeStruct((NK, FRAMES, KC), bf16),
            jax.ShapeDtypeStruct((NK, ROWS, KC), bf16),
        ),
        in_specs=[hbm] * 2,
        out_specs=(vmem,) * 3,
        scratch_shapes=[
            pltpu.VMEM((NK, FRAMES, KC), jnp.int32),
            pltpu.VMEM((NB, FRAMES, BS), f32),
            pltpu.VMEM((ROWS, 128), f32),
            pltpu.VMEM((rs_slots, OWN, BS), f32),
            pltpu.VMEM((NB, OWN, BS), f32),
            pltpu.VMEM((NB, OWN, BS), f32),
            pltpu.VMEM((NZ, NB, OWN, BS), bf16),
            pltpu.VMEM((1, 128), f32),
            pltpu.VMEM((NORIENT, 1, 128), f32),
            pltpu.VMEM((1, 128), f32),
            pltpu.VMEM((NZ, 1, 128), f32),
            pltpu.VMEM((ROWS, FRAMES), f32),
            dma((NK,)),
            dma((NK,)),
            dma,
            dma((rs_slots,)),
            dma,
            dma((NB,)),
            dma,
            dma,
            dma,
            dma,
            dma,
            dma,
        ],
        compiler_params=pltpu.CompilerParams(
            collective_id=0, has_side_effects=True, vmem_limit_bytes=40 * 1024 * 1024
        ),
    )(model, patterns)
    return pl.pallas_call(
        update_kernel,
        name="update",
        out_shape=jax.ShapeDtypeStruct((ROWS, COLS), bf16),
        in_specs=[vmem] * 3,
        out_specs=hbm,
        scratch_shapes=[pltpu.VMEM((NU, ROWS, UC), bf16), dma((NU,))],
        compiler_params=pltpu.CompilerParams(vmem_limit_bytes=30 * 1024 * 1024),
    )(probs, counts, held)


def solution(mesh):
    placed = (P("orient", "pix"), P(None, "pix"))
    return jax.shard_map(
        on_device, mesh=mesh, in_specs=placed, out_specs=P("orient", "pix"), check_vma=False
    )
```

```python
import math

import jax
import jax.numpy as jnp
from jax import lax
from jax.experimental import pallas as pl
from jax.experimental.pallas import tpu as pltpu
from jax.sharding import PartitionSpec as P

PIX = 65536
BETA = 2.0 / math.sqrt(PIX)
MESH = pl.DeviceIdType.MESH

ROWS = 768
COLS = 4096
FRAMES = 384
KC = 512
NK = COLS // KC
NB = 3
BS = ROWS // NB
NZ = 8
OWN = FRAMES // NZ
NORIENT = 16

RS_HOPS = (((4, 3), (3, 4)) * 3)[:3]


def exchange_kernel(
    model_ref,
    pat_ref,
    probs_ref,
    cb,
    mv,
    pv,
    part,
    tot,
    recv,
    y_out,
    y_in,
    all_e,
    stat_own,
    stat_all,
    fac_own,
    fac_all,
    turned,
    pat_sem,
    mod_sem,
    rs_send,
    rs_recv,
    y_send,
    y_recv,
    ag_send,
    ag_recv,
    st_send,
    st_recv,
    fc_send,
    fc_recv,
):
    o = lax.axis_index("orient")
    p = lax.axis_index("pix")
    y = p // NZ
    z = lax.rem(p, NZ)

    def at_z(dz):
        return (o, y * NZ + lax.rem(z + dz + NZ, NZ))

    y_peer = (o, (1 - y) * NZ + z)
    far_first = (11, 10, 9, 8, 7, 6, 5, 14, 15, 13, 12, 4, 3, 2, 1)
    orient_peers = [(do, (lax.rem(o + do, NORIENT), p)) for do in far_first]

    def pat_copy(k):
        return pltpu.make_async_copy(
            pat_ref.at[:, pl.ds(k * KC, KC)], pv.at[k], pat_sem.at[k]
        )

    def mod_copy(k):
        return pltpu.make_async_copy(
            model_ref.at[:, pl.ds(k * KC, KC)], mv.at[k], mod_sem.at[k]
        )

    for k in range(NK):
        pat_copy(k).start()
        mod_copy(k).start()

    barrier = pltpu.get_barrier_semaphore()
    for dz in range(1, NZ):
        pl.semaphore_signal(barrier, inc=1, device_id=at_z(dz), device_id_type=MESH)
    pl.semaphore_signal(barrier, inc=1, device_id=y_peer, device_id_type=MESH)
    for _, peer in orient_peers:
        pl.semaphore_signal(barrier, inc=1, device_id=peer, device_id_type=MESH)

    def own_part(b, c):
        row = pl.multiple_of(lax.rem(c + NZ, NZ) * OWN, 8)
        return part.at[b, pl.ds(row, OWN), :]

    def rs_slot(b, way, step):
        return sum(sum(h) for h in RS_HOPS[:b]) + (RS_HOPS[b][0] if way else 0) + step - 1

    def rs_copy(b, way, step):
        hops = RS_HOPS[b][way]
        sign = 1 if way else -1
        slot = rs_slot(b, way, step)
        left = hops - step + 1
        src = own_part(b, z + sign * left) if step == 1 else recv.at[slot - 1]
        return pltpu.make_async_remote_copy(
            src_ref=src,
            dst_ref=recv.at[slot],
            send_sem=rs_send,
            recv_sem=rs_recv.at[slot],
            device_id=at_z(sign),
            device_id_type=MESH,
        )

    def rs_start(b):
        for way in range(2):
            rs_copy(b, way, 1).start()

    def rs_step(b, step):
        for way in range(2):
            hops = RS_HOPS[b][way]
            if step > hops:
                continue
            rs_copy(b, way, step).wait_recv()
            if step < hops:
                sign = 1 if way else -1
                slot = rs_slot(b, way, step)
                recv[slot] += own_part(b, z + sign * (hops - step))[...]
                rs_copy(b, way, step + 1).start()

    def y_copy(b):
        return pltpu.make_async_remote_copy(
            src_ref=y_out.at[b],
            dst_ref=y_in.at[b],
            send_sem=y_send,
            recv_sem=y_recv.at[b],
            device_id=y_peer,
            device_id_type=MESH,
        )

    def rs_end(b):
        low = recv[rs_slot(b, 0, RS_HOPS[b][0])]
        high = recv[rs_slot(b, 1, RS_HOPS[b][1])]
        y_out[b] = own_part(b, z)[...] + (low + high)
        y_copy(b).start()

    ones = jnp.ones((8, 128), jnp.float32)

    def chunk(k, carry):
        mod_copy(k).wait()
        pat_copy(k).wait()
        c = pv[k].astype(jnp.float32).astype(jnp.bfloat16)
        cb[k] = c
        x = mv[k].astype(jnp.float32)
        t = tot[...]
        for j in range(KC // 128):
            t = t + x[:, j * 128 : (j + 1) * 128]
        tot[...] = t
        logs = jnp.log(x)
        hi = logs.astype(jnp.bfloat16)
        lo = (logs - hi.astype(jnp.float32)).astype(jnp.bfloat16)
        twice = jnp.concatenate([c, c], axis=1)
        d = lax.dot_general(
            twice,
            jnp.concatenate([hi, lo], axis=1),
            (((1,), (1,)), ((), ())),
            preferred_element_type=jnp.float32,
        )
        for b in range(NB):
            part[b] += d[:, b * BS : (b + 1) * BS]
        return carry

    def finish():
        row = lax.dot_general(
            ones,
            tot[...],
            (((1,), (1,)), ((), ())),
            precision=lax.Precision.HIGHEST,
            preferred_element_type=jnp.float32,
        )
        for b in range(NB):
            part[b] -= row[0:1, b * BS : (b + 1) * BS]
            act(("start", b))

    tail = [("step", b, step) for step in range(1, 4) for b in range(NB)]
    for b in range(NB):
        tail += [("step", b, 4), ("end", b)]

    def act(hook):
        kind, b = hook[0], hook[1]
        if kind == "start":
            if b == 0:
                pl.semaphore_wait(barrier, NZ + len(orient_peers))
            rs_start(b)
        elif kind == "step":
            rs_step(b, hook[2])
        else:
            rs_end(b)

    tot[...] = jnp.zeros_like(tot)
    part[...] = jnp.zeros_like(part)
    lax.fori_loop(0, NK, chunk, 0)
    finish()
    for hook in tail:
        act(hook)

    def ag_copy(b, dz):
        return pltpu.make_async_remote_copy(
            src_ref=all_e.at[z, b],
            dst_ref=all_e.at[z, b],
            send_sem=ag_send,
            recv_sem=ag_recv,
            device_id=at_z(dz),
            device_id_type=MESH,
        )

    scores = []
    for b in range(NB):
        y_copy(b).wait_recv()
        scores.append(BETA * (y_out[b] + y_in[b]))
    top = scores[0]
    for b in range(1, NB):
        top = jnp.maximum(top, scores[b])
    m = jnp.max(top, axis=1, keepdims=True)
    acc = jnp.zeros((OWN, BS), jnp.float32)
    for b in range(NB):
        e = jnp.exp(scores[b] - m)
        acc = acc + e
        all_e[z, b] = e.astype(jnp.bfloat16)
    esum = jnp.sum(acc, axis=1, keepdims=True)
    row = lax.broadcasted_iota(jnp.int32, (OWN, 128), 0)
    lane = lax.broadcasted_iota(jnp.int32, (OWN, 128), 1)
    stat_own[...] = jnp.sum(
        jnp.where(lane == row, m, jnp.where(lane == row + 64, esum, 0.0)), axis=0, keepdims=True
    )

    def stat_copy(do, peer):
        return pltpu.make_async_remote_copy(
            src_ref=stat_own,
            dst_ref=stat_all.at[NORIENT - do - 1],
            send_sem=st_send,
            recv_sem=st_recv,
            device_id=peer,
            device_id_type=MESH,
        )

    for do, peer in orient_peers:
        stat_copy(do, peer).start()
    for b in range(NB):
        for dz in (4, 3, 5, 2, 6, 1, 7):
            ag_copy(b, dz).start()

    stat_all[NORIENT - 1] = stat_own[...]
    stats_sent = stat_all.at[pl.ds(0, NORIENT - 1)]
    pltpu.make_async_copy(stats_sent, stats_sent, st_recv).wait()
    stats = stat_all[:, 0, :]
    big = jnp.max(stats, axis=0, keepdims=True)
    weight = jnp.exp(stats - big)
    whole = jnp.sum(pltpu.roll(stats, 64, 1) * weight, axis=0, keepdims=True)
    used = lax.broadcasted_iota(jnp.int32, (1, 128), 1) < OWN
    fac_own[...] = jnp.where(used, jnp.exp(stat_own[...] - big) / jnp.where(used, whole, 1.0), 0.0)

    def fac_copy(dz):
        return pltpu.make_async_remote_copy(
            src_ref=fac_own,
            dst_ref=fac_all.at[z],
            send_sem=fc_send,
            recv_sem=fc_recv,
            device_id=at_z(dz),
            device_id_type=MESH,
        )

    for dz in (4, 3, 5, 2, 6, 1, 7):
        fac_copy(dz).start()
    fac_all[z] = fac_own[...]

    e_sent = all_e.at[pl.ds(0, NZ - 1)]
    fac_sent = fac_all.at[pl.ds(0, NZ - 1)]
    pltpu.make_async_copy(e_sent, e_sent, ag_recv).wait()
    for b in range(NB):
        block = jnp.concatenate([all_e[zz, b].astype(jnp.float32) for zz in range(NZ)], axis=0)
        turned[b * BS : (b + 1) * BS, :] = block.T

    pltpu.make_async_copy(fac_sent, fac_sent, fc_recv).wait()
    pad = jnp.zeros((1, FRAMES - 128), jnp.float32)
    factors = jnp.zeros((1, FRAMES), jnp.float32)
    for zz in range(NZ):
        piece = jnp.concatenate([fac_all[zz], pad], axis=1)
        factors = factors + (pltpu.roll(piece, zz * OWN, 1) if zz else piece)
    for b in range(NB):
        rows = slice(b * BS, (b + 1) * BS)
        probs_ref[rows, :] = (turned[rows, :] * factors).astype(jnp.bfloat16)

    pltpu.make_async_copy(recv, recv, rs_send).wait()
    pltpu.make_async_copy(y_out, y_out, y_send).wait()
    pltpu.make_async_copy(e_sent, e_sent, ag_send).wait()
    pltpu.make_async_copy(stats_sent, stats_sent, st_send).wait()
    pltpu.make_async_copy(fac_sent, fac_sent, fc_send).wait()


NU = 8
UC = COLS // NU


def update_kernel(probs_ref, counts_ref, held_ref, out_ref, done, sem):
    norm = jnp.sum(probs_ref[...].astype(jnp.float32), axis=1, keepdims=True)
    inv = jnp.broadcast_to(1.0 / (norm + 1.0), (ROWS, 128))
    scale = jnp.concatenate([inv] * (UC // 128), axis=1)

    def put(u):
        return pltpu.make_async_copy(done.at[u], out_ref.at[:, pl.ds(u * UC, UC)], sem.at[u])

    for u in range(NU):
        k, c = divmod(u * UC, KC)
        num = jnp.dot(
            probs_ref[...], counts_ref[k, :, c : c + UC], preferred_element_type=jnp.float32
        )
        for b in range(NB):
            rows = slice(b * BS, (b + 1) * BS)
            x = held_ref[k, rows, c : c + UC].astype(jnp.float32)
            done[u, rows, :] = ((num[rows] + x) * scale[rows]).astype(jnp.bfloat16)
        put(u).start()
    for u in range(NU):
        put(u).wait()


def on_device(model, patterns):
    f32, bf16 = jnp.float32, jnp.bfloat16
    dma = pltpu.SemaphoreType.DMA
    vmem = pl.BlockSpec(memory_space=pltpu.VMEM)
    hbm = pl.BlockSpec(memory_space=pltpu.HBM)
    rs_slots = sum(sum(h) for h in RS_HOPS)
    probs, counts, held = pl.pallas_call(
        exchange_kernel,
        name="exchange",
        out_shape=(
            jax.ShapeDtypeStruct((ROWS, FRAMES), bf16),
            jax.ShapeDtypeStruct((NK, FRAMES, KC), bf16),
            jax.ShapeDtypeStruct((NK, ROWS, KC), bf16),
        ),
        in_specs=[hbm] * 2,
        out_specs=(vmem,) * 3,
        scratch_shapes=[
            pltpu.VMEM((NK, FRAMES, KC), jnp.int32),
            pltpu.VMEM((NB, FRAMES, BS), f32),
            pltpu.VMEM((ROWS, 128), f32),
            pltpu.VMEM((rs_slots, OWN, BS), f32),
            pltpu.VMEM((NB, OWN, BS), f32),
            pltpu.VMEM((NB, OWN, BS), f32),
            pltpu.VMEM((NZ, NB, OWN, BS), bf16),
            pltpu.VMEM((1, 128), f32),
            pltpu.VMEM((NORIENT, 1, 128), f32),
            pltpu.VMEM((1, 128), f32),
            pltpu.VMEM((NZ, 1, 128), f32),
            pltpu.VMEM((ROWS, FRAMES), f32),
            dma((NK,)),
            dma((NK,)),
            dma,
            dma((rs_slots,)),
            dma,
            dma((NB,)),
            dma,
            dma,
            dma,
            dma,
            dma,
            dma,
        ],
        compiler_params=pltpu.CompilerParams(
            collective_id=0, has_side_effects=True, vmem_limit_bytes=40 * 1024 * 1024
        ),
    )(model, patterns)
    return pl.pallas_call(
        update_kernel,
        name="update",
        out_shape=jax.ShapeDtypeStruct((ROWS, COLS), bf16),
        in_specs=[vmem] * 3,
        out_specs=hbm,
        scratch_shapes=[pltpu.VMEM((NU, ROWS, UC), bf16), dma((NU,))],
        compiler_params=pltpu.CompilerParams(vmem_limit_bytes=30 * 1024 * 1024),
    )(probs, counts, held)


def solution(mesh):
    placed = (P("orient", "pix"), P(None, "pix"))
    return jax.shard_map(
        on_device, mesh=mesh, in_specs=placed, out_specs=P("orient", "pix"), check_vma=False
    )
```
